32 devices in a mesh: dp: 4 (over y, core), expert: 8 (over z, x).
Axes of the slice: x: 2, y: 2, z: 4, core: 2. Of those that a mesh axis runs over, the one named last changes fastest.
Arguments:
- tokens: bfloat16 [5120, 2048], P(('dp', 'expert')), may hold values from -6 to 6
- cotangent: bfloat16 [5120, 2048], P(('dp', 'expert')), may hold values from -6 to 6
- routes: int32 [5120, 6], P(('dp', 'expert')), may hold values from 0 to 15, all different within a row; in each aligned block of 160 rows (0 to 159, 160 to 319, ...) at most 64 rows name the same one
- route_weight: bfloat16 [5120, 6], P(('dp', 'expert')), may hold values from 0.049804688 to 0.3984375
- cont_segment: int32 [4, 256], P('dp'), may hold values from 0 to 3, never falling along the last dimension, each value on 1 to 128 neighbouring positions
- attn_gain: bfloat16 [2048], P('expert'), may hold values from 0.25 to 1.75
- kv_gain: bfloat16 [512], P('expert'), may hold values from 0.25 to 1.75
- ffn_gain: bfloat16 [2048], P('expert'), may hold values from 0.25 to 1.75
- query_weight: bfloat16 [2048, 3072], P('expert'), may hold values from -0.125 to 0.125
- latent_weight: bfloat16 [2048, 576], P('expert'), may hold values from -0.125 to 0.125
- expand_weight: bfloat16 [512, 4096], P('expert'), may hold values from -0.5 to 0.5
- output_weight: bfloat16 [2048, 2048], P('expert'), may hold values from -0.75 to 0.75
- shared_gate: bfloat16 [2048, 2816], P(None, 'expert'), may hold values from -0.125 to 0.125
- shared_up: bfloat16 [2048, 2816], P(None, 'expert'), may hold values from -0.125 to 0.125
- shared_down: bfloat16 [2816, 2048], P('expert'), may hold values from -0.109375 to 0.109375
- expert_gate: bfloat16 [16, 2048, 1408], P('expert'), may hold values from -0.125 to 0.125
- expert_up: bfloat16 [16, 2048, 1408], P('expert'), may hold values from -0.125 to 0.125
- expert_down: bfloat16 [16, 1408, 2048], P('expert'), may hold values from -0.15625 to 0.15625
Outputs:
- block_out: bfloat16 [5120, 2048], P(('dp', 'expert'))
- input_grad: float32 [5120, 2048], P(('dp', 'expert'))
- attn_gain_grad: float32 [2048], P(('dp', 'expert'))
- kv_gain_grad: float32 [512], P(('dp', 'expert'))
- ffn_gain_grad: float32 [2048], P(('dp', 'expert'))
- query_weight_grad: float32 [2048, 3072], P(('dp', 'expert'))
- latent_weight_grad: float32 [2048, 576], P(('dp', 'expert'))
- expand_weight_grad: float32 [512, 4096], P(('dp', 'expert'))
- output_weight_grad: float32 [2048, 2048], P(('dp', 'expert'))
- shared_gate_grad: float32 [2048, 2816], P('dp', 'expert')
- shared_up_grad: float32 [2048, 2816], P('dp', 'expert')
- shared_down_grad: float32 [2816, 2048], P('expert', 'dp')
- expert_gate_grad: float32 [16, 2048, 1408], P('expert', 'dp')
- expert_up_grad: float32 [16, 2048, 1408], P('expert', 'dp')
- expert_down_grad: float32 [16, 1408, 2048], P('expert', None, 'dp')
The draws below stay inside these ranges and needn't reach their ends.
Inputs may be any that keep to these rules, and one draw needn't show every extreme that they name: `routes`: each row names 6 different experts; within the rows of one device (aligned blocks of 160 rows) no expert is named by more than 64 rows. `cont_segment`: each row numbers the 4 continuations of one group in order, never falling; each continuation has 1 to 128 tokens, the longest exactly 128.
All inputs are finite; a program needn't handle non-finite values.
Results may differ from the reference program's by a relative error of at most 0.02.
Values may be sent and summed in bfloat16 or wider, within the bound.
No kernel may reach another device: no remote copies, remote signals or barrier semaphores. Data moves between devices by JAX's collectives and lax.ppermute only.
A program may use at most 384 MiB of HBM per device.

```python
import math
import jax
import jax.numpy as jnp
import numpy as np
from jax import lax

D = 2048
HEADS = 16
NOPE = 128
ROPE = 64
KVR = 512
VDIM = 128
FFE = 1408
FFS = 2816
TOP = 6
PLEN = 1024
CLEN = 128
CONT_TOK = 256
CONTS = 4
EXPERTS = 16
GROUP_TOK = 1280
TOK_DEV = 160
TOKENS = 5120
CAP = 64
N_DP = 4


def levels(stream_key, shape, split, low, top_value):
    factor_of, own = 1.0, jax.random.fold_in(stream_key, 6)
    for position, blocks in split:
        heights = jnp.exp(jax.random.uniform(jax.random.fold_in(own, position), (blocks,), jnp.float32, low / len(split), top_value / len(split)))
        factor_of = factor_of * jnp.repeat(heights, shape[position] // blocks).reshape([-1 if axis == position else 1 for axis in range(len(shape))])
    return factor_of


def profile(amount, total, reach, lean):
    loads = [(1 << 20) // math.isqrt(standing ** lean) + 1 for standing in range(2, amount + 1)]
    rest, given = total - reach - (amount - 1), [1] * (amount - 1)
    while rest > 0:
        candidates = [i for i in range(amount - 1) if given[i] < reach]
        whole, remaining = sum([loads[i] for i in candidates]), rest
        for i in candidates:
            addition = min(reach - given[i], max(1, remaining * loads[i] // whole), rest)
            given[i] = given[i] + addition
            rest = rest - addition
    return np.array([reach] + given)


def uneven_parts(own_key, count, total, most, skew):
    if count == 2:
        one = jax.random.randint(own_key, (), max(1, total - most), min(most, total - 1) + 1)
        return jnp.stack([one, total - one])
    tallies = jnp.asarray(profile(count, total, most, skew), jnp.int32)
    twos = (count - 1) // 2
    donor, receiver = tallies[1:1 + 2 * twos:2], tallies[2:2 + 2 * twos:2]
    slack = jnp.minimum(donor - 1, most - receiver)
    moved = jax.random.randint(jax.random.fold_in(own_key, 1), (twos,), 0, 1 << 20) % (slack + 1)
    tallies = tallies.at[1:1 + 2 * twos:2].set(donor - moved).at[2:2 + 2 * twos:2].set(receiver + moved)
    return tallies[jax.random.permutation(jax.random.fold_in(own_key, 2), count)]


def assign_block(rng, own, number, rows, number_of, top, most, lean):
    order = jax.random.permutation(rng, number_of)
    packed, ordinary = shares(number_of, rows * top, most, lean, True), shares(number_of, rows * top, most, lean, False)
    places = jnp.arange(number_of)

    def named(tallies, turn):
        used = int((tallies > 0).sum())
        fixed = max(1, used // 4)
        shifted = fixed + (places - fixed + turn * (used - fixed)) % max(1, number_of - fixed)
        return jnp.zeros((number_of,), jnp.int32).at[order[jnp.where(places < fixed, places, shifted)]].set(jnp.asarray(tallies, jnp.int32))

    tallies = jnp.where(number % 4 == 0, named(packed, number // 4), named(ordinary, number - number // 4 - 1))
    mixed = jax.random.permutation(jax.random.fold_in(own, 3), number_of)
    donor, taker = mixed[0:number_of // 2 * 2:2], mixed[1:number_of // 2 * 2:2]
    room = jnp.minimum(tallies[donor] - 1, most - tallies[taker]) // 2
    room = jnp.where((donor == order[0]) | (taker == order[0]) | (tallies[taker] == 0), 0, jnp.maximum(room, 0))
    shifted = jax.random.randint(jax.random.fold_in(own, 4), (number_of // 2,), 0, 1 << 20) % (room + 1)
    tallies = tallies.at[donor].add(-shifted).at[taker].add(shifted)
    members = jnp.searchsorted(jnp.cumsum(tallies), jnp.arange(rows * top), side="right").astype(jnp.int32)
    table = members.reshape(top, rows).T
    table = table[jax.random.permutation(jax.random.fold_in(own, 1), rows)]
    turn = jax.random.randint(jax.random.fold_in(own, 2), (rows, 1), 0, top)
    return jnp.take_along_axis(table, (jnp.arange(top)[None, :] + turn) % top, axis=1)


def shares(amount, total, bound, lean, full):
    portions = [(1 << 20) // math.isqrt(rank ** lean) + 1 for rank in range(1, amount + 1)]
    largest = bound if full else min(bound, max(-(-total // amount), total * portions[0] // sum(portions)))
    least = 1 if total - largest >= amount - 1 else 0
    holding, spare = [largest] + [least] * (amount - 1), total - largest - least * (amount - 1)
    while spare > 0:
        movable = [i for i in range(1, amount) if holding[i] < largest] or [i for i in range(1, amount) if holding[i] < bound]
        whole, remaining = sum([portions[i] for i in movable]), spare
        for i in movable:
            more = min(bound - holding[i], max(1, remaining * portions[i] // whole), spare)
            holding[i] = holding[i] + more
            spare = spare - more
    return np.array(holding)


def scatter_about(stream_key, extent, deviation, most, split=(), held_as=jnp.bfloat16):
    result = deviation * jax.random.normal(stream_key, extent, jnp.float32)
    if split:
        result = result * levels(stream_key, extent, split, -0.22, 0.18)
    return jnp.clip(result, -most, most).astype(held_as)


def setup_inputs(seed: int = 0) -> dict:
    key_of = jax.random.split(jax.random.key(seed), 19)
    tokens = scatter_about(key_of[0], (TOKENS, D), 1.0, 6.0, ((0, 32),))
    cotangent = scatter_about(key_of[1], (TOKENS, D), 1.0, 6.0, ((0, 32),))
    routes_keys = jax.random.split(jax.random.fold_in(key_of[2], 1), TOKENS // TOK_DEV)
    routes_turns = jax.random.permutation(jax.random.fold_in(key_of[2], 3), TOKENS // TOK_DEV)
    routes = jax.vmap(lambda own, number: assign_block(jax.random.fold_in(key_of[2], 2), own, number, TOK_DEV, EXPERTS, TOP, CAP, 1))(routes_keys, routes_turns).reshape((TOKENS, TOP))
    route_weight = jnp.clip(jnp.exp(math.log(0.3984375) - 2.0794415 * jax.random.uniform(key_of[3], (TOKENS, TOP), jnp.float32) ** levels(key_of[3], (TOKENS, TOP), ((0, 32),), -0.2, 0.2)), 0.049804688, 0.3984375).astype(jnp.bfloat16)
    cont_segment = jax.vmap(lambda own: jnp.searchsorted(jnp.cumsum(uneven_parts(own, CONTS, CONT_TOK, CLEN, 1)), jnp.arange(CONT_TOK), side="right"))(jax.random.split(key_of[4], N_DP)).reshape((N_DP, CONT_TOK)).astype(jnp.int32)
    attn_gain = jnp.clip(1.0 + 0.15 * jax.random.normal(key_of[5], (D,), jnp.float32), 0.25, 1.75).astype(jnp.bfloat16)
    kv_gain = jnp.clip(1.0 + 0.15 * jax.random.normal(key_of[6], (KVR,), jnp.float32), 0.25, 1.75).astype(jnp.bfloat16)
    ffn_gain = jnp.clip(1.0 + 0.15 * jax.random.normal(key_of[7], (D,), jnp.float32), 0.25, 1.75).astype(jnp.bfloat16)
    query_weight = scatter_about(key_of[8], (D, HEADS * (NOPE + ROPE)), D ** -0.5, 0.125, ((0, 8),))
    latent_weight = scatter_about(key_of[9], (D, KVR + ROPE), D ** -0.5, 0.125, ((0, 8),))
    expand_weight = scatter_about(key_of[10], (KVR, HEADS * (NOPE + VDIM)), (KVR // 4) ** -0.5, 0.5, ((0, 8),))
    output_weight = scatter_about(key_of[11], (HEADS * VDIM, D), (HEADS * VDIM // 32) ** -0.5, 0.75, ((0, 8),))
    shared_gate = scatter_about(key_of[12], (D, FFS), D ** -0.5, 0.125, ((1, 8),))
    shared_up = scatter_about(key_of[13], (D, FFS), D ** -0.5, 0.125, ((1, 8),))
    shared_down = scatter_about(key_of[14], (FFS, D), FFS ** -0.5, 0.109375, ((0, 8),))
    expert_gate = scatter_about(key_of[15], (EXPERTS, D, FFE), D ** -0.5, 0.125, ((0, 8),))
    expert_up = scatter_about(key_of[16], (EXPERTS, D, FFE), D ** -0.5, 0.125, ((0, 8),))
    expert_down = scatter_about(key_of[17], (EXPERTS, FFE, D), FFE ** -0.5, 0.15625, ((0, 8),))
    return dict(tokens=tokens, cotangent=cotangent, routes=routes, route_weight=route_weight, cont_segment=cont_segment, attn_gain=attn_gain, kv_gain=kv_gain, ffn_gain=ffn_gain, query_weight=query_weight, latent_weight=latent_weight, expand_weight=expand_weight, output_weight=output_weight, shared_gate=shared_gate, shared_up=shared_up, shared_down=shared_down, expert_gate=expert_gate, expert_up=expert_up, expert_down=expert_down)


EPSILON = 1e-06
MASK_FILL = -1e+30
EXACT = lax.Precision.HIGHEST

@jax.custom_vjp
def low(v):
    return lax.optimization_barrier(v.astype(jnp.bfloat16)).astype(jnp.float32)

@jax.custom_vjp
def low_back(v):
    return v

def low_keep(v):
    return (low(v), None)

def low_pass(kept, grad):
    return (grad,)

def back_keep(v):
    return (v, None)

def back_low(kept, grad):
    return (low(grad),)
low.defvjp(low_keep, low_pass)
low_back.defvjp(back_keep, back_low)

def matmul(left, right):
    return jnp.dot(left, right, precision=EXACT, preferred_element_type=jnp.float32)

def norm_rows(values, gain_vec):
    return values * lax.rsqrt(lax.optimization_barrier(jnp.mean(values * values, axis=-1, keepdims=True)) + EPSILON) * gain_vec

def rope_tables(positions, rot_width):
    half_width = rot_width // 2
    frequency = jnp.exp(jnp.arange(half_width, dtype=jnp.float32) * (-2.0 * math.log(10000.0) / rot_width))
    angles = positions.astype(jnp.float32)[:, None] * frequency[None, :]
    return (jnp.cos(angles), jnp.sin(angles))

def rotate(values, cos_table, sin_table):
    half_width = values.shape[-1] // 2
    lower_half = values[..., :half_width]
    upper_half = values[..., half_width:]
    return jnp.concatenate([lower_half * cos_table - upper_half * sin_table, upper_half * cos_table + lower_half * sin_table], axis=-1)

def group_layout(segment_row):
    cont_len = segment_row.shape[0]
    earlier = lax.optimization_barrier(jnp.sum((segment_row[None, :] < segment_row[:, None]).astype(jnp.int32), axis=1))
    offsets = jnp.arange(cont_len, dtype=jnp.int32) - earlier
    positions = jnp.concatenate([jnp.arange(PLEN, dtype=jnp.int32), (PLEN + offsets).astype(jnp.int32)])
    sequence = jnp.concatenate([jnp.zeros((PLEN,), jnp.int32), (segment_row + 1).astype(jnp.int32)])
    return (positions, sequence)

def attend_group(parts):
    query_latent, query_rope, latent_keys, rope_keys, sequence = parts
    key_index = jnp.arange(GROUP_TOK, dtype=jnp.int32)
    visible = (key_index[None, :] <= key_index[:, None]) & ((sequence[None, :] == sequence[:, None]) | (sequence[None, :] == 0))
    score_scale = 1.0 / math.sqrt(NOPE + ROPE)
    raw = jnp.einsum('thr,sr->hts', query_latent, latent_keys, precision=EXACT)
    raw = raw + jnp.einsum('thp,sp->hts', query_rope, rope_keys, precision=EXACT)
    scores = low_back(raw * score_scale)
    probs = jax.nn.softmax(jnp.where(visible[None, :, :], scores, MASK_FILL), axis=-1)
    probs_low = low(probs)
    return low_back(low(jnp.einsum('hts,sr->thr', probs_low, latent_keys, precision=EXACT)))

def forward(inputs, attn_gain, kv_gain, ffn_gain, query_weight, latent_weight, expand_weight, output_weight, shared_gate, shared_up, shared_down, expert_gate, expert_up, expert_down, mixing, cos_table, sin_table, seq_table):
    hidden_one = low(norm_rows(inputs, attn_gain))
    queries = low_back(low(matmul(hidden_one, query_weight))).reshape(TOKENS, HEADS, NOPE + ROPE)
    compressed = low_back(matmul(hidden_one, latent_weight))
    latent_keys = low(norm_rows(compressed[:, :KVR], kv_gain))
    rope_keys = low(rotate(compressed[:, KVR:], cos_table, sin_table))
    expand = expand_weight.reshape(KVR, HEADS, NOPE + VDIM)
    query_latent = low_back(low(jnp.einsum('thn,rhn->thr', queries[:, :, :NOPE], expand[:, :, :NOPE], precision=EXACT)))
    query_rope = low(rotate(queries[:, :, NOPE:], cos_table[:, None, :], sin_table[:, None, :]))
    grouped = (query_latent.reshape(N_DP, GROUP_TOK, HEADS, KVR), query_rope.reshape(N_DP, GROUP_TOK, HEADS, ROPE), latent_keys.reshape(N_DP, GROUP_TOK, KVR), rope_keys.reshape(N_DP, GROUP_TOK, ROPE), seq_table)
    out_latent = lax.map(jax.checkpoint(attend_group), grouped).reshape(TOKENS, HEADS, KVR)
    head_out = low_back(low(jnp.einsum('thr,rhv->thv', out_latent, expand[:, :, NOPE:], precision=EXACT)))
    head_out = head_out.reshape(TOKENS, HEADS * VDIM)
    resid = inputs + low_back(matmul(head_out, output_weight))
    hidden_two = low(norm_rows(resid, ffn_gain))
    shared_gate_pre = low_back(matmul(hidden_two, shared_gate))
    shared_up_pre = low_back(matmul(hidden_two, shared_up))
    shared_out = low_back(matmul(low(jax.nn.silu(shared_gate_pre) * shared_up_pre), shared_down))

    def expert_step(routed, parts):
        gate_weight, up_weight, down_weight, column = parts
        gate_pre = low_back(matmul(hidden_two, gate_weight))
        up_pre = low_back(matmul(hidden_two, up_weight))
        expert_out = low_back(low(matmul(low(jax.nn.silu(gate_pre) * up_pre), down_weight)))
        return (routed + column[:, None] * expert_out, None)
    routed, unused = lax.scan(expert_step, jnp.zeros((TOKENS, D), jnp.float32), (expert_gate, expert_up, expert_down, mixing.T))
    return resid + shared_out + routed

def reference(tokens, cotangent, routes, route_weight, cont_segment, attn_gain, kv_gain, ffn_gain, query_weight, latent_weight, expand_weight, output_weight, shared_gate, shared_up, shared_down, expert_gate, expert_up, expert_down):
    positions, seq_table = jax.vmap(group_layout)(cont_segment)
    cos_table, sin_table = rope_tables(positions.reshape(-1), ROPE)
    weight_f = route_weight.astype(jnp.float32)
    expert_ids = jnp.arange(EXPERTS, dtype=jnp.int32)
    mixing = jnp.zeros((TOKENS, EXPERTS), jnp.float32)
    for slot_k in range(TOP):
        mixing = mixing + weight_f[:, slot_k:slot_k + 1] * (routes[:, slot_k:slot_k + 1] == expert_ids[None, :]).astype(jnp.float32)

    def closed(inputs, gain_a, gain_k, gain_f, weight_q, weight_l, weight_e, weight_o, weight_sg, weight_su, weight_sd, weight_eg, weight_eu, weight_ed):
        return forward(inputs, gain_a, gain_k, gain_f, weight_q, weight_l, weight_e, weight_o, weight_sg, weight_su, weight_sd, weight_eg, weight_eu, weight_ed, mixing, cos_table, sin_table, seq_table)
    out, pullback = jax.vjp(closed, tokens.astype(jnp.float32), attn_gain.astype(jnp.float32), kv_gain.astype(jnp.float32), ffn_gain.astype(jnp.float32), query_weight.astype(jnp.float32), latent_weight.astype(jnp.float32), expand_weight.astype(jnp.float32), output_weight.astype(jnp.float32), shared_gate.astype(jnp.float32), shared_up.astype(jnp.float32), shared_down.astype(jnp.float32), expert_gate.astype(jnp.float32), expert_up.astype(jnp.float32), expert_down.astype(jnp.float32))
    grads = pullback(cotangent.astype(jnp.float32))
    return (out.astype(jnp.bfloat16), grads[0], grads[1], grads[2], grads[3], grads[4], grads[5], grads[6], grads[7], grads[8], grads[9], grads[10], grads[11], grads[12], grads[13])
```

```python
import math

import jax
import jax.numpy as jnp
from jax import lax
from jax.sharding import PartitionSpec as P

D = 2048
HEADS = 16
NOPE = 128
ROPE = 64
KVR = 512
VDIM = 128
TOP = 6
EXP_DEV = 2
PLEN = 1024


EPSILON = 1e-06
MASK_FILL = -1e30


def rms_scale(values):
    return lax.rsqrt(jnp.mean(values * values, axis=-1, keepdims=True) + EPSILON)


def norm_back(gradient, values, inv_rms, gain_vec):
    weighted = gradient * gain_vec
    return inv_rms * weighted - values * (inv_rms * inv_rms * inv_rms) * jnp.mean(
        weighted * values, axis=-1, keepdims=True
    )


def rope_tables(positions, rot_width):
    half_width = rot_width // 2
    frequency = jnp.exp(
        jnp.arange(half_width, dtype=jnp.float32) * (-2.0 * math.log(10000.0) / rot_width)
    )
    angles = positions.astype(jnp.float32)[:, None] * frequency[None, :]
    return (jnp.cos(angles), jnp.sin(angles))


def rotate(values, cos_table, sin_table):
    half_width = values.shape[-1] // 2
    lower_half = values[..., :half_width]
    upper_half = values[..., half_width:]
    return jnp.concatenate(
        [
            lower_half * cos_table - upper_half * sin_table,
            upper_half * cos_table + lower_half * sin_table,
        ],
        axis=-1,
    )


def rotate_back(gradient, cos_table, sin_table):
    half_width = gradient.shape[-1] // 2
    lower_half = gradient[..., :half_width]
    upper_half = gradient[..., half_width:]
    return jnp.concatenate(
        [
            lower_half * cos_table + upper_half * sin_table,
            upper_half * cos_table - lower_half * sin_table,
        ],
        axis=-1,
    )


def group_layout(segment_row, prompt_len):
    cont_len = segment_row.shape[0]
    earlier = jnp.sum((segment_row[None, :] < segment_row[:, None]).astype(jnp.int32), axis=1)
    offsets = jnp.arange(cont_len, dtype=jnp.int32) - earlier
    positions = jnp.concatenate([jnp.arange(prompt_len, dtype=jnp.int32), prompt_len + offsets])
    sequence = jnp.concatenate([jnp.zeros((prompt_len,), jnp.int32), segment_row + 1])
    return (positions, sequence)


def norm_parts(values):
    inv = rms_scale(values)
    return values * inv, inv


def expert_ring(size):
    return [*range(0, size, 2), *range(size - 1, 0, -2)]


class Ring:
    def __init__(self):
        self.size = lax.axis_size("expert")
        order = expert_ring(self.size)
        following = [(order[i], order[(i + 1) % self.size]) for i in range(self.size)]
        self.forward = following
        self.backward = [(b, a) for a, b in following]
        index = lax.axis_index("expert")
        self.place = jnp.where(index % 2 == 0, index // 2, self.size - 1 - index // 2)

    def owner(self, offset):
        place = (self.place + offset) % self.size
        return jnp.where(place < self.size // 2, 2 * place, 2 * (self.size - 1 - place) + 1)

    def ahead(self, value):
        return lax.ppermute(value, "expert", self.forward)

    def back(self, value):
        return lax.ppermute(value, "expert", self.backward)


def ring_gather(ring, block):
    rows, cols = block.shape
    half = cols // 2
    buffer = jnp.zeros((ring.size, rows, cols), block.dtype)
    buffer = lax.dynamic_update_slice(buffer, block[None], (ring.owner(0), 0, 0))
    fore = hind = block
    for step in range(1, ring.size // 2):
        fore, hind = ring.ahead(fore), ring.back(hind)
        buffer = lax.dynamic_update_slice(buffer, fore[None], (ring.owner(-step), 0, 0))
        buffer = lax.dynamic_update_slice(buffer, hind[None], (ring.owner(step), 0, 0))
    fore, hind = ring.ahead(fore[:, :half]), ring.back(hind[:, half:])
    far = ring.owner(ring.size // 2)
    buffer = lax.dynamic_update_slice(buffer, fore[None], (far, 0, 0))
    return lax.dynamic_update_slice(buffer, hind[None], (far, 0, half))


def ring_reduce(ring, chunk, cols, streams):
    width = cols // streams
    half = width // 2
    pieces = []
    for stream in range(streams):
        low, mid, high = stream * width, stream * width + half, (stream + 1) * width
        far = ring.owner(ring.size // 2)
        fore = ring.ahead(chunk(far, low, mid).astype(jnp.bfloat16))
        hind = ring.back(chunk(far, mid, high).astype(jnp.bfloat16))
        for step in range(ring.size // 2 - 1, 0, -1):
            ahead, behind = ring.owner(step), ring.owner(-step)
            if step == ring.size // 2 - 1:
                fore = jnp.concatenate([fore, jnp.zeros_like(fore)], axis=1)
                hind = jnp.concatenate([jnp.zeros_like(hind), hind], axis=1)
            fore = chunk(ahead, low, high) + fore.astype(jnp.float32)
            hind = chunk(behind, low, high) + hind.astype(jnp.float32)
            fore = ring.ahead(fore.astype(jnp.bfloat16))
            hind = ring.back(hind.astype(jnp.bfloat16))
        own = chunk(ring.owner(0), low, high)
        pieces.append(own + fore.astype(jnp.float32) + hind.astype(jnp.float32))
    return jnp.concatenate(pieces, axis=1)


def pick_bit(value, axis, groups, bit):
    shape = value.shape
    chunk = shape[axis] // groups
    split = value.reshape(*shape[:axis], groups // 2, 2, chunk, *shape[axis + 1 :])
    taken = lax.dynamic_index_in_dim(split, bit, axis + 1, keepdims=False)
    return taken.reshape(*shape[:axis], shape[axis] // 2, *shape[axis + 1 :])


def dp_bits():
    count = lax.axis_size("dp")
    index = lax.axis_index("dp")
    return [(index >> level) & 1 for level in range(count.bit_length() - 1)]


def dp_swap(value, level):
    count = lax.axis_size("dp")
    return lax.ppermute(value, "dp", [(i, i ^ (1 << level)) for i in range(count)])


def dp_reduce(piece, operand, operand_axis, axis):
    bits = dp_bits()
    groups = lax.axis_size("dp")
    arrived = []
    for level, bit in enumerate(bits):
        outgoing = piece(pick_bit(operand, operand_axis, groups, 1 - bit))
        for value in arrived:
            outgoing = outgoing + pick_bit(value, axis, groups, 1 - bit).astype(jnp.float32)
        operand = pick_bit(operand, operand_axis, groups, bit)
        arrived = [pick_bit(value, axis, groups, bit) for value in arrived]
        arrived.append(dp_swap(outgoing.astype(jnp.bfloat16), level))
        groups //= 2
    total = piece(operand)
    for value in arrived:
        total = total + value.astype(jnp.float32)
    return total


def dp_gather(block):
    stack = block[None]
    for level, bit in enumerate(dp_bits()):
        other = dp_swap(stack, level)
        first = jnp.where(bit == 0, stack, other)
        second = jnp.where(bit == 0, other, stack)
        stack = jnp.concatenate([first, second], axis=0)
    return stack


def full_sum(value):
    size = lax.axis_size("expert")
    index = lax.axis_index("expert")
    width = size
    while width > 1:
        width //= 2
        bit = (index // width) % 2
        split = value.reshape(value.shape[0], 2, width, value.shape[-1])
        kept = lax.dynamic_index_in_dim(split, bit, 1, keepdims=False)
        sent = lax.dynamic_index_in_dim(split, 1 - bit, 1, keepdims=False)
        value = kept + lax.ppermute(sent, "expert", [(i, i ^ width) for i in range(size)])
    value = value[:, 0, :]
    groups = lax.axis_size("dp")
    for level, bit in enumerate(dp_bits()):
        kept = pick_bit(value, 0, groups, bit)
        value = kept + dp_swap(pick_bit(value, 0, groups, 1 - bit), level)
        groups //= 2
    return value[0]


def dot(left, right, left_axis, right_axis):
    return lax.dot_general(
        left, right, (((left_axis,), (right_axis,)), ((), ())), preferred_element_type=jnp.float32
    )


def silu_parts(gate_pre, up_pre, d_act):
    sigma = jax.nn.sigmoid(gate_pre)
    act = (gate_pre * sigma * up_pre).astype(jnp.bfloat16)
    d_gate = (d_act * up_pre * sigma * (1.0 + gate_pre * (1.0 - sigma))).astype(jnp.bfloat16)
    d_up = (d_act * gate_pre * sigma).astype(jnp.bfloat16)
    return act, d_gate, d_up


def body(
    tokens,
    cotangent,
    routes,
    route_weight,
    cont_segment,
    attn_gain,
    kv_gain,
    ffn_gain,
    query_weight,
    latent_weight,
    expand_weight,
    output_weight,
    shared_gate,
    shared_up,
    shared_down,
    expert_gate,
    expert_up,
    expert_down,
):
    low = jnp.bfloat16
    ring = Ring()
    size = ring.size
    count = lax.axis_size("dp")
    mine = lax.axis_index("expert")
    tok_rows = tokens.shape[0]
    group_rows = tok_rows * size
    heads = HEADS // size
    head_width = NOPE + ROPE
    expert_count = EXP_DEV * size
    slot_cap = min(tok_rows, (tok_rows * TOP * 16 // (15 * expert_count) + 7) // 8 * 8)
    score_scale = 1.0 / math.sqrt(NOPE + ROPE)
    row_start = mine * tok_rows

    def own_rows(value):
        return lax.dynamic_slice_in_dim(value, row_start, tok_rows, 0)

    share = lax.axis_index("dp")

    def my_share(weight):
        rows = weight.shape[0] // count
        return lax.dynamic_slice_in_dim(weight, share * rows, rows, 0)

    tokens_all = ring_gather(ring, tokens).reshape(group_rows, D)
    small = jnp.concatenate([attn_gain, kv_gain, ffn_gain])[None]
    gains = ring_gather(ring, small)[:, 0, :]
    attn_gain_f = gains[:, : attn_gain.shape[0]].reshape(-1).astype(jnp.float32)
    kv_gain_f = gains[:, attn_gain.shape[0] : -ffn_gain.shape[0]].reshape(-1).astype(jnp.float32)
    ffn_gain_f = gains[:, -ffn_gain.shape[0] :].reshape(-1).astype(jnp.float32)

    query_share = my_share(query_weight)
    query_share = query_share.reshape(-1, size, heads * head_width).transpose(1, 0, 2)
    expand_share = my_share(expand_weight)
    expand_share = expand_share.reshape(-1, size, heads * (NOPE + VDIM)).transpose(1, 0, 2)
    query_cols = lax.all_to_all(query_share, "expert", 0, 0)
    expand_cols = lax.all_to_all(expand_share, "expert", 0, 0)
    latent_rows = ring_gather(ring, my_share(latent_weight))

    def whole_rows(part):
        stack = dp_gather(part)
        return stack.transpose(1, 0, 2, 3).reshape(-1, stack.shape[-1])

    query_own = whole_rows(query_cols)
    latent_full = whole_rows(latent_rows)
    expand_own = whole_rows(expand_cols).reshape(KVR, heads, NOPE + VDIM)
    key_part = expand_own[:, :, :NOPE]
    value_part = expand_own[:, :, NOPE:]

    grads_all = ring_gather(ring, cotangent)
    route_pack = jnp.concatenate([routes.astype(low), route_weight], axis=1)
    route_all = ring_gather(ring, route_pack)

    positions, sequence = group_layout(cont_segment[0], PLEN)
    cos_all, sin_all = rope_tables(positions, ROPE)
    key_index = jnp.arange(group_rows, dtype=jnp.int32)
    visible = (key_index[None, :] <= key_index[:, None]) & (
        (sequence[None, :] == sequence[:, None]) | (sequence[None, :] == 0)
    )
    normed_all, unused = norm_parts(tokens_all.astype(jnp.float32))
    hidden_one = (normed_all * attn_gain_f).astype(low)
    queries = dot(hidden_one, query_own, 1, 0).astype(low).reshape(group_rows, heads, head_width)
    compressed = dot(hidden_one, latent_full, 1, 0)
    latent_raw_all = compressed[:, :KVR]
    latent_normed_all, unused = norm_parts(latent_raw_all)
    latent_keys = (latent_normed_all * kv_gain_f).astype(low)
    rope_keys = rotate(compressed[:, KVR:], cos_all, sin_all).astype(low)
    query_latent = jnp.einsum(
        "thn,rhn->htr", queries[:, :, :NOPE], key_part, preferred_element_type=jnp.float32
    ).astype(low)
    query_rope = rotate(
        queries[:, :, NOPE:].astype(jnp.float32), cos_all[:, None, :], sin_all[:, None, :]
    ).astype(low)
    query_rope = query_rope.transpose(1, 0, 2)

    def masked_scores():
        raw = jnp.einsum(
            "htr,sr->hts", query_latent, latent_keys, preferred_element_type=jnp.float32
        )
        raw = raw + jnp.einsum(
            "htp,sp->hts", query_rope, rope_keys, preferred_element_type=jnp.float32
        )
        return jnp.where(visible[None, :, :], raw * score_scale, MASK_FILL)

    scores = masked_scores()
    top_score = jnp.max(scores, axis=-1, keepdims=True)
    exp_terms = jnp.exp(scores - top_score)
    row_total = jnp.sum(exp_terms, axis=-1, keepdims=True)
    log_total = top_score + jnp.log(row_total)
    probs_low = (exp_terms / row_total).astype(low)
    out_latent = jnp.einsum(
        "hts,sr->htr", probs_low, latent_keys, preferred_element_type=jnp.float32
    ).astype(low)
    head_out = jnp.einsum(
        "htr,rhv->thv", out_latent, value_part, preferred_element_type=jnp.float32
    ).astype(low)
    head_out = head_out.reshape(group_rows, heads * VDIM)

    def rows_of(value, owner):
        return lax.dynamic_slice_in_dim(value, owner * tok_rows, tok_rows, 0)

    inputs = tokens.astype(jnp.float32)
    resid = inputs + ring_reduce(
        ring,
        lambda owner, lo, hi: dot(rows_of(head_out, owner), output_weight[:, lo:hi], 1, 0),
        D,
        2,
    )
    normed_two, inv_two = norm_parts(resid)
    hidden_two = (normed_two * ffn_gain_f).astype(low)
    hidden_all = ring_gather(ring, hidden_two)

    routes_all = route_all[:, :, :TOP]
    weight_all = route_all[:, :, TOP:]
    upto = (
        jnp.arange(tok_rows, dtype=jnp.int32)[:, None]
        <= jnp.arange(tok_rows, dtype=jnp.int32)[None, :]
    ).astype(low)
    slot = jnp.arange(slot_cap, dtype=jnp.float32)[None, :, None]
    grads_flat = grads_all.reshape(group_rows, D)
    hidden_flat = hidden_all.reshape(group_rows, D)
    picks, weighted_picks, expert_outs, expert_backs, expert_grads = [], [], [], [], []
    for which in range(EXP_DEV):
        name = (mine * EXP_DEV + which).astype(low)
        hit = routes_all == name
        named = jnp.any(hit, axis=2)
        weight = jnp.sum(jnp.where(hit, weight_all, jnp.zeros((), low)).astype(jnp.float32), axis=2)
        rank = dot(named.astype(low), upto, 1, 0) - 1.0
        chosen = (rank[:, None, :] == slot) & named[:, None, :]
        pick = chosen.astype(low)
        weighted_pick = jnp.where(chosen, weight[:, None, :], 0.0).astype(low)
        arrived = jnp.einsum(
            "sct,std->scd", pick, hidden_all, preferred_element_type=jnp.float32
        ).astype(low).reshape(size * slot_cap, D)
        arrived_grads = jnp.einsum(
            "sct,std->scd", weighted_pick, grads_all, preferred_element_type=jnp.float32
        ).astype(low).reshape(size * slot_cap, D)
        d_act = dot(arrived_grads, expert_down[which], 1, 1)
        gate_pre = dot(arrived, expert_gate[which], 1, 0)
        up_pre = dot(arrived, expert_up[which], 1, 0)
        act, d_gate, d_up = silu_parts(gate_pre, up_pre, d_act)
        d_rows = dot(d_gate, expert_gate[which], 1, 1) + dot(d_up, expert_up[which], 1, 1)
        expert_out = dot(act, expert_down[which], 1, 0).astype(low)
        picks.append(pick)
        weighted_picks.append(weighted_pick)
        expert_outs.append(expert_out.reshape(size, slot_cap, D))
        expert_backs.append(d_rows.astype(low).reshape(size, slot_cap, D))
        expert_grads.append((arrived, arrived_grads, act, d_gate, d_up))

    d_shared_act = dot(grads_flat, shared_down, 1, 1)
    shared_gate_pre = dot(hidden_flat, shared_gate, 1, 0)
    shared_up_pre = dot(hidden_flat, shared_up, 1, 0)
    shared_act, d_shared_gate, d_shared_up = silu_parts(
        shared_gate_pre, shared_up_pre, d_shared_act
    )

    def at(value, owner):
        return lax.dynamic_index_in_dim(value, owner, 0, keepdims=False)

    def back_chunk(owner, lo, hi):
        term = dot(rows_of(d_shared_gate, owner), shared_gate[lo:hi], 1, 1)
        term = term + dot(rows_of(d_shared_up, owner), shared_up[lo:hi], 1, 1)
        for pick, rows in zip(picks, expert_backs, strict=True):
            term = term + dot(at(pick, owner), at(rows, owner)[:, lo:hi], 0, 0)
        return term

    d_hidden_two = ring_reduce(ring, back_chunk, D, 2)

    def out_chunk(owner, lo, hi):
        term = dot(rows_of(shared_act, owner), shared_down[:, lo:hi], 1, 0)
        for pick, rows in zip(weighted_picks, expert_outs, strict=True):
            term = term + dot(at(pick, owner), at(rows, owner)[:, lo:hi], 0, 0)
        return term

    block_out = (resid + ring_reduce(ring, out_chunk, D, 2)).astype(low)

    gate_grads, up_grads, down_grads = [], [], []
    for arrived, arrived_grads, act, d_gate, d_up in expert_grads:
        down_grads.append(
            dp_reduce(lambda part, act=act: dot(act, part, 0, 0), arrived_grads, 1, 1)
        )
        gate_grads.append(
            dp_reduce(lambda part, d_gate=d_gate: dot(part, d_gate, 0, 0), arrived, 1, 0)
        )
        up_grads.append(dp_reduce(lambda part, d_up=d_up: dot(part, d_up, 0, 0), arrived, 1, 0))
    shared_down_grad = dp_reduce(lambda part: dot(shared_act, part, 0, 0), grads_flat, 1, 1)
    shared_gate_grad = dp_reduce(lambda part: dot(part, d_shared_gate, 0, 0), hidden_flat, 1, 0)
    shared_up_grad = dp_reduce(lambda part: dot(part, d_shared_up, 0, 0), hidden_flat, 1, 0)

    grad_ffn_gain = jnp.sum(d_hidden_two * normed_two, axis=0)
    d_resid = cotangent.astype(jnp.float32) + norm_back(d_hidden_two, resid, inv_two, ffn_gain_f)
    d_attn = d_resid.astype(low)
    d_attn_all = ring_gather(ring, d_attn).reshape(group_rows, D)

    d_head = dot(d_attn_all, output_weight, 1, 1).astype(low).reshape(group_rows, heads, VDIM)
    d_out_latent = jnp.einsum(
        "thv,rhv->htr", d_head, value_part, preferred_element_type=jnp.float32
    ).astype(low)
    probs = jnp.exp(masked_scores() - log_total)
    probs_again = probs.astype(low)
    d_probs = jnp.einsum(
        "htr,sr->hts", d_out_latent, latent_keys, preferred_element_type=jnp.float32
    )
    row_delta = jnp.sum(probs * d_probs, axis=-1, keepdims=True)
    d_scores = (probs * (d_probs - row_delta)).astype(low)
    d_latent_keys = score_scale * jnp.einsum(
        "hts,htr->sr", d_scores, query_latent, preferred_element_type=jnp.float32
    )
    d_latent_keys = d_latent_keys + jnp.einsum(
        "hts,htr->sr", probs_again, d_out_latent, preferred_element_type=jnp.float32
    )
    d_rope_keys = score_scale * jnp.einsum(
        "hts,htp->sp", d_scores, query_rope, preferred_element_type=jnp.float32
    )
    d_query_latent = (
        score_scale
        * jnp.einsum("hts,sr->htr", d_scores, latent_keys, preferred_element_type=jnp.float32)
    ).astype(low)
    d_query_rope = score_scale * jnp.einsum(
        "hts,sp->thp", d_scores, rope_keys, preferred_element_type=jnp.float32
    )
    d_query_nope = jnp.einsum(
        "htr,rhn->thn", d_query_latent, key_part, preferred_element_type=jnp.float32
    )
    d_query_pe = rotate_back(d_query_rope, cos_all[:, None, :], sin_all[:, None, :])
    d_queries = (
        jnp.concatenate([d_query_nope, d_query_pe], axis=-1)
        .astype(low)
        .reshape(group_rows, heads * head_width)
    )
    d_keys = jnp.concatenate([d_latent_keys, d_rope_keys], axis=-1)
    own_keys_grad = ring_reduce(
        ring, lambda owner, lo, hi: rows_of(d_keys[:, lo:hi], owner), KVR + ROPE, 1
    )
    d_hidden_one = ring_reduce(
        ring,
        lambda owner, lo, hi: dot(rows_of(d_queries, owner), query_own[lo:hi], 1, 1),
        D,
        2,
    )
    own_latent_grad = own_keys_grad[:, :KVR]
    latent_raw = own_rows(latent_raw_all)
    latent_normed, inv_latent = norm_parts(latent_raw)
    grad_kv_gain = jnp.sum(own_latent_grad * latent_normed, axis=0)
    d_latent_raw = norm_back(own_latent_grad, latent_raw, inv_latent, kv_gain_f)
    d_rope_raw = rotate_back(own_keys_grad[:, KVR:], own_rows(cos_all), own_rows(sin_all))
    d_compressed = jnp.concatenate([d_latent_raw, d_rope_raw], axis=-1).astype(low)
    d_hidden_one = d_hidden_one + dot(d_compressed, latent_full, 1, 1)
    normed_one, inv_one = norm_parts(inputs)
    grad_attn_gain = jnp.sum(d_hidden_one * normed_one, axis=0)
    input_grad = d_resid + norm_back(d_hidden_one, inputs, inv_one, attn_gain_f)
    d_compressed_all = ring_gather(ring, d_compressed).reshape(group_rows, KVR + ROPE)

    grad_query = dp_reduce(lambda part: dot(part, d_queries, 0, 0), hidden_one, 1, 0)
    grad_query = lax.all_to_all(grad_query.astype(low).reshape(size, -1, heads * head_width), "expert", 0, 0)
    grad_query = grad_query.transpose(1, 0, 2).reshape(-1, HEADS * head_width).astype(jnp.float32)
    grad_key = jnp.einsum(
        "htr,thn->rhn", d_query_latent, queries[:, :, :NOPE], preferred_element_type=jnp.float32
    )
    grad_value = jnp.einsum(
        "htr,thv->rhv", out_latent, d_head, preferred_element_type=jnp.float32
    )
    grad_expand = jnp.concatenate([grad_key, grad_value], axis=-1).reshape(KVR, -1)
    grad_expand = dp_reduce(lambda part: part, grad_expand, 0, 0)
    grad_expand = lax.all_to_all(
        grad_expand.astype(low).reshape(size, -1, heads * (NOPE + VDIM)), "expert", 0, 0
    )
    grad_expand = grad_expand.transpose(1, 0, 2).reshape(-1, HEADS * (NOPE + VDIM))
    grad_expand = grad_expand.astype(jnp.float32)
    grad_output = dp_reduce(lambda part: dot(part, d_attn_all, 0, 0), head_out, 1, 0)
    grad_output = lax.ppermute(
        grad_output,
        ("dp", "expert"),
        [(j * size + e, count * e + j) for j in range(count) for e in range(size)],
    )
    latent_cols = hidden_one.reshape(group_rows, count, size, D // (count * size))
    latent_cols = lax.dynamic_index_in_dim(latent_cols, mine, 2, keepdims=False)
    latent_cols = latent_cols.reshape(group_rows, D // size)
    grad_latent = dp_reduce(lambda part: dot(part, d_compressed_all, 0, 0), latent_cols, 1, 0)
    gain_grads = full_sum(
        jnp.concatenate(
            [
                grad_attn_gain.reshape(count, size, -1),
                grad_ffn_gain.reshape(count, size, -1),
                grad_kv_gain.reshape(count, size, -1),
            ],
            axis=2,
        )
    )
    width = D // (count * size)
    return (
        block_out,
        input_grad,
        gain_grads[:width],
        gain_grads[2 * width :],
        gain_grads[width : 2 * width],
        grad_query,
        grad_latent,
        grad_expand,
        grad_output,
        shared_gate_grad,
        shared_up_grad,
        shared_down_grad,
        jnp.stack(gate_grads),
        jnp.stack(up_grads),
        jnp.stack(down_grads),
    )


def solution(mesh):
    placed = (
        P(("dp", "expert"), None),
        P(("dp", "expert"), None),
        P(("dp", "expert"), None),
        P(("dp", "expert"), None),
        P("dp", None),
        P("expert"),
        P("expert"),
        P("expert"),
        P("expert", None),
        P("expert", None),
        P("expert", None),
        P("expert", None),
        P(None, "expert"),
        P(None, "expert"),
        P("expert", None),
        P("expert", None, None),
        P("expert", None, None),
        P("expert", None, None),
    )
    return jax.shard_map(
        body,
        mesh=mesh,
        in_specs=placed,
        out_specs=(
            P(("dp", "expert"), None),
            P(("dp", "expert"), None),
            P(("dp", "expert")),
            P(("dp", "expert")),
            P(("dp", "expert")),
            P(("dp", "expert"), None),
            P(("dp", "expert"), None),
            P(("dp", "expert"), None),
            P(("dp", "expert"), None),
            P("dp", "expert"),
            P("dp", "expert"),
            P("expert", "dp"),
            P("expert", "dp", None),
            P("expert", "dp", None),
            P("expert", None, "dp"),
        ),
        check_vma=False,
    )
```
